32 devices in a mesh: row: 8 (over z, core), col: 4 (over y, x).
Axes of the slice: x: 2, y: 2, z: 4, core: 2. Of those that a mesh axis runs over, the one named last changes fastest.
Arguments:
- amplitudes: bfloat16 [256, 4, 16384], P('col', None, 'row'), may hold values from -6 to 6
- integrals: bfloat16 [4, 16384, 16384], P(None, 'row', 'col'), may hold values from -0.046875 to 0.046875
- block_sizes: int32 [4], replicated, may hold values from 8192 to 16384, as said below
Outputs:
- ladder: float32 [256, 4, 16384], P('row', None, 'col')
The draws below stay inside these ranges and needn't reach their ends.
Inputs may be any that keep to these rules, and one draw needn't show every extreme that they name: Each irrep block uses its first block_sizes[h] pairs; in every draw some block uses all 16384.
All inputs are finite; a program needn't handle non-finite values.
Results may differ from the reference program's by a relative error of at most 0.0003.
Values may be sent and summed in bfloat16 or wider, within the bound.
A program may use at most 128 MiB of HBM per device.

```python
import jax
import jax.numpy as jnp

NIRR = 4
P_SIZE = 16384
NPAIR = 256


def draw_block_sizes(key, part):
    first, second = jax.random.split(jax.random.fold_in(key, 7))
    sizes = jax.random.randint(first, (NIRR,), P_SIZE // 2, P_SIZE + 1)
    chosen = jax.random.randint(second, (), 0, NIRR)
    full = jnp.full((NIRR,), P_SIZE, jnp.int32)
    return jnp.where(jnp.arange(NIRR) == chosen, full, sizes).astype(jnp.int32)


def levels(stream_key, dims, shards, low, largest):
    gain, own = 1.0, jax.random.fold_in(stream_key, 6)
    for dim, blocks in shards:
        draws = jnp.exp(jax.random.uniform(jax.random.fold_in(own, dim), (blocks,), jnp.float32, low / len(shards), largest / len(shards)))
        gain = gain * jnp.repeat(draws, dims[dim] // blocks).reshape([-1 if axis == dim else 1 for axis in range(len(dims))])
    return gain


def scatter_about(stream_key, shape, spread, limit, shards=(), kind=jnp.bfloat16):
    level = levels(stream_key, shape, shards, -0.22, 0.18) if shards else 1.0
    result = jax.random.normal(stream_key, shape, jnp.float32) * spread * level
    return jnp.minimum(jnp.maximum(result, -limit), limit).astype(kind)


def setup_inputs(seed: int = 0) -> dict:
    key_of = jax.random.split(jax.random.key(seed), 4)
    amplitudes = scatter_about(key_of[0], (NPAIR, NIRR, P_SIZE), 1.0, 6.0, ((0, 4), (2, 8)))
    integrals = scatter_about(key_of[1], (NIRR, P_SIZE, P_SIZE), P_SIZE ** -0.5, 0.046875, ((1, 8), (2, 4)))
    block_sizes = draw_block_sizes(jax.random.fold_in(key_of[3], 71), 0)
    return dict(amplitudes=amplitudes, integrals=integrals, block_sizes=block_sizes)


def reference(amplitudes, integrals, block_sizes):
    columns = jnp.arange(P_SIZE, dtype=jnp.int32)
    blocks = []
    for irrep in range(NIRR):
        live = columns < block_sizes[irrep]
        masked = jnp.where(live[None, :], amplitudes[:, irrep, :], jnp.zeros((), amplitudes.dtype))
        total = jnp.dot(masked, integrals[irrep], preferred_element_type=jnp.float32)
        blocks.append(jnp.where(live[None, :], total, jnp.zeros((), jnp.float32)))
    return jnp.stack(blocks, 1)
```

```python
import functools
import math

import jax
import jax.numpy as jnp
from jax import lax
from jax.experimental import pallas as pl
from jax.experimental.pallas import tpu as pltpu
from jax.sharding import PartitionSpec as P

CORES = 2
CHUNK = 512
SLOTS = 8
LANES = 128
LAG = 3
RING = 2 * LAG + 6
TOP = 32766.0
TINY = 1e-30


def kernel(chips, cols, steps, chunk, sizes, amp, integ, out, raw, gathered, panel, part, peer, stage, inbox,
           scale_out, scale_in, raw_sem, gather_send, gather_recv, panel_sem, peer_send, peer_recv,
           stage_send, inbox_recv, scale_send, scale_recv):
    row, col = lax.axis_index("row"), lax.axis_index("col")
    z, core = row // CORES, row % CORES
    share, blocks, span = amp.shape
    pairs = share // CORES
    per_block = steps // blocks
    slots, peers, ring = panel.shape[0], peer.shape[0], stage.shape[0]
    early = min(per_block, slots)
    width = chunk * per_block
    mate = z * CORES + 1 - core
    side = math.isqrt(cols)
    shifts = sorted(((a, b) for a in range(side) for b in range(side) if a or b), key=lambda s: (sum(map(bool, s)), s))

    def partner(shift, sign):
        a, b = (sign * s + side for s in shift)
        return (col // side + a) % side * side + (col % side + b) % side

    def send(src, dst, send_sem, recv_sem, to_row, to_col):
        return pltpu.make_async_remote_copy(
            src_ref=src, dst_ref=dst, send_sem=send_sem, recv_sem=recv_sem,
            device_id={"row": to_row, "col": to_col}, device_id_type=pl.DeviceIdType.MESH)

    def panel_copy(t):
        lanes = pl.ds(pl.multiple_of((t % per_block) * chunk, chunk), chunk)
        slot = t % slots
        return pltpu.make_async_copy(integ.at[t // per_block, :, lanes], panel.at[slot], panel_sem.at[slot])

    raw_copy = pltpu.make_async_copy(amp, raw, raw_sem)

    def gather_copy(h, q, to_col):
        return send(gathered.at[h, q, col], gathered.at[h, q, col], gather_send, gather_recv.at[h, q], row, to_col)

    def peer_copy(t):
        slot = t % peers
        return send(part.at[t, 1 - core], peer.at[slot], peer_send.at[slot], peer_recv.at[slot], mate, col)

    def data_copy(t, way, count, to_row, first):
        slot = t % ring
        return send(stage.at[slot, pl.ds(first, count)], inbox.at[slot, pl.ds(first + 1 - way, count)],
                    stage_send.at[way, slot], inbox_recv.at[way, slot], to_row, col)

    def scale_copy(t, way, to_row):
        slot = t % ring
        return send(scale_out.at[way, slot], scale_in.at[way, slot], scale_send.at[way, slot],
                    scale_recv.at[way, slot], to_row, col)

    def loop(low, high, body):
        lax.fori_loop(low, high, lambda i, c: (body(i), c)[1], 0)

    def when(condition, body, *args):
        @pl.when(condition)
        def _():
            body(*args)

    raw_copy.start()
    for t in range(min(slots, steps)):
        panel_copy(t).start()

    barrier = pltpu.get_barrier_semaphore()

    def greet(to_row, to_col):
        pl.semaphore_signal(barrier, inc=1, device_id={"row": to_row, "col": to_col},
                            device_id_type=pl.DeviceIdType.MESH)

    for shift in shifts:
        greet(row, partner(shift, 1))
    greet(mate, col)
    when(z > 0, greet, row - CORES, col)
    when(z < chips - 1, greet, row + CORES, col)

    def mask(h):
        index = row * span + lax.broadcasted_iota(jnp.int32, (share, span), 1)
        values = jnp.where(index < sizes[h], raw[:, h, :].astype(jnp.float32), 0.0)
        values = values.astype(gathered.dtype)
        for q in range(CORES):
            gathered[h, q, col] = values[q * pairs:(q + 1) * pairs]

    raw_copy.wait()
    mask(0)
    pl.semaphore_wait(barrier, cols + jnp.where(z > 0, 1, 0) + jnp.where(z < chips - 1, 1, 0))

    def scatter(h):
        def one(q):
            for shift in shifts:
                gather_copy(h, q, partner(shift, 1)).start()

        loop(0, CORES, one)

    scatter(0)

    for h in range(1, blocks):
        mask(h)
        scatter(h)

    def collect(h, q):
        others = gathered.at[h, q, pl.ds(0, cols - 1)]
        pltpu.make_async_copy(others, others, gather_recv.at[h, q]).wait()

    def next_panel(t):
        when(t + slots < steps, lambda: panel_copy(t + slots).start())

    def start_peer(t):
        when(t >= peers, lambda: peer_copy(t - peers).wait_send())
        peer_copy(t).start()

    def half(t, q):
        when(t == 0, collect, 0, q)
        when(q == 0, lambda: panel_copy(t).wait())
        left = gathered[0, q].reshape(cols * pairs, span)
        value = jnp.dot(left, panel[t % slots], preferred_element_type=jnp.float32)
        part[t, q] = value.reshape(chips, pairs, chunk)
        when(core != q, start_peer, t)
        when(q == 1, next_panel, t)

    def full(t):
        h = t // per_block
        when(t % per_block == 0, lambda: loop(0, CORES, lambda q: collect(h, q)))
        panel_copy(t).wait()
        left = gathered[h].reshape(CORES * cols * pairs, span)
        value = jnp.dot(left, panel[t % slots], preferred_element_type=jnp.float32)
        part[t] = value.reshape(CORES, chips, pairs, chunk)
        start_peer(t)
        next_panel(t)

    def combine(t):
        peer_copy(t).wait_recv()

        def add(d):
            part[t, core, d] = part[t, core, d] + peer[t % peers, d]

        loop(0, chips, add)

    def fold(value):
        value = jnp.abs(value)
        value = functools.reduce(jnp.maximum, [value[i:i + 8] for i in range(0, pairs, 8)])
        return functools.reduce(jnp.maximum, [value[:, i:i + LANES] for i in range(0, chunk, LANES)])

    def spread(value):
        return jnp.concatenate([value] * (chunk // LANES), axis=1)

    def ahead_of(way):
        return jnp.where(way == 0, chips - 1 - z, z)

    def each_count(count, low, high, body):
        for n in range(low, high):
            when(count == n, body, n)

    def sent_wait(t, way):
        scale_copy(t, way, row).wait_send()
        each_count(ahead_of(way), 1, chips, lambda n: data_copy(t, way, n, row, 0).wait_send())

    def relay(t, way):
        up = way == 0
        has_source = jnp.where(up, z, chips - 1 - z) > 0
        ahead = ahead_of(way)
        to_row = row + CORES - 2 * CORES * way
        first = jnp.where(up, z + 1, 0)
        slot = t % ring

        @pl.when(has_source)
        def _():
            scale_copy(t, way, row).wait_recv()
            each_count(ahead + 1, 1, chips, lambda n: data_copy(t, way, n, row, 0).wait_recv())

        def take(d):
            factor = spread(scale_in[way, slot])
            part[t, core, d] = part[t, core, d] + inbox[slot, d + 1 - way].astype(jnp.int32).astype(jnp.float32) * factor

        when(jnp.logical_and(has_source, ahead > 0), loop, first, first + ahead, take)

        @pl.when(ahead > 0)
        def _():
            when(t >= ring, sent_wait, t - ring, way)
            largest = lax.fori_loop(
                first, first + ahead, lambda d, m: jnp.maximum(m, fold(part[t, core, d])), jnp.full((8, LANES), TINY, jnp.float32))
            largest = jnp.max(largest, axis=0, keepdims=True)
            scale_out[way, slot] = largest * (1.0 / TOP)
            scale_copy(t, way, to_row).start()
            inverse = spread(TOP / largest)

            def put(d):
                stage[slot, d] = jnp.round(part[t, core, d] * inverse).astype(jnp.int32).astype(jnp.int16)

            loop(first, first + ahead, put)
            each_count(ahead, 1, chips, lambda n: data_copy(t, way, n, to_row, first).start())

        when(has_source, take, z)

    def finish(t):
        h = t // per_block
        low = (t % per_block) * chunk
        index = col * width + low + lax.broadcasted_iota(jnp.int32, (pairs, chunk), 1)
        out[:, h, pl.ds(pl.multiple_of(low, chunk), chunk)] = jnp.where(index < sizes[h], part[t, core, z], 0.0)

    def at(j, body):
        ahead = jnp.logical_and(core == 0, j < early)
        t = jnp.where(ahead, j, jnp.where(jnp.logical_and(core == 0, j < 2 * early), -1, j - early))
        when(jnp.logical_and(t >= 0, t < steps), body, t)

    near = jnp.where(2 * z < chips, 0, 1)
    short = jnp.where(2 * z < chips, z, chips - 1 - z)
    near_lag = 1 + LAG * short
    far_lag = 1 + LAG * (chips - 1 - short)
    end_lag = 1 + LAG * (chips - 1)

    def step(i):
        when(jnp.logical_and(i < 2 * early, i != early), lambda: half(i % early, i // early))
        when(jnp.logical_and(i >= 2 * early, i < steps + early), lambda: full(i - early))
        at(i - 1, combine)
        at(i - near_lag, lambda t: relay(t, near))
        at(i - far_lag, lambda t: relay(t, 1 - near))
        at(i - end_lag, finish)
        when(i == early, lambda: half(0, 1))

    loop(0, steps + early + end_lag, step)

    everything = gathered.at[:, :, pl.ds(0, cols - 1)]
    pltpu.make_async_copy(everything, everything, gather_send).wait()
    loop(max(0, steps - peers), steps, lambda t: peer_copy(t).wait_send())

    def drain(t):
        for way in range(2):
            when(ahead_of(way) > 0, sent_wait, t, way)

    loop(max(0, steps - ring), steps, drain)


def body(chips, cols, amplitudes, integrals, block_sizes):
    share, blocks, span = amplitudes.shape
    width = integrals.shape[2]
    chunk = min(CHUNK, width)
    steps = blocks * (width // chunk)
    total = share * cols
    pairs = total // (chips * CORES)
    assert share == CORES * pairs and chips == cols
    slots = min(SLOTS, steps)
    peers = min(2 * SLOTS, steps)
    ring = min(RING, steps)
    dma = pltpu.SemaphoreType.DMA
    result = pl.pallas_call(
        functools.partial(kernel, chips, cols, steps, chunk),
        out_shape=jax.ShapeDtypeStruct((pairs, blocks, width), jnp.float32),
        in_specs=[
            pl.BlockSpec(memory_space=pltpu.SMEM),
            pl.BlockSpec(memory_space=pl.ANY),
            pl.BlockSpec(memory_space=pl.ANY),
        ],
        out_specs=pl.BlockSpec(memory_space=pltpu.VMEM),
        scratch_shapes=[
            pltpu.VMEM((share, blocks, span), amplitudes.dtype),
            pltpu.VMEM((blocks, CORES, cols, pairs, span), amplitudes.dtype),
            pltpu.VMEM((slots, span, chunk), integrals.dtype),
            pltpu.VMEM((steps, CORES, chips, pairs, chunk), jnp.float32),
            pltpu.VMEM((peers, chips, pairs, chunk), jnp.float32),
            pltpu.VMEM((ring, chips, pairs, chunk), jnp.int16),
            pltpu.VMEM((ring, chips + 1, pairs, chunk), jnp.int16),
            pltpu.VMEM((2, ring, 1, LANES), jnp.float32),
            pltpu.VMEM((2, ring, 1, LANES), jnp.float32),
            dma,
            dma,
            dma((blocks, CORES)),
            dma((slots,)),
            dma((peers,)),
            dma((peers,)),
            dma((2, ring)),
            dma((2, ring)),
            dma((2, ring)),
            dma((2, ring)),
        ],
        compiler_params=pltpu.CompilerParams(
            collective_id=0, has_side_effects=True, vmem_limit_bytes=63 * 2**20
        ),
        name="ladder",
    )(block_sizes, amplitudes, integrals)
    return result


def solution(mesh):
    placed = (P("col", None, "row"), P(None, "row", "col"), P())
    return jax.shard_map(
        functools.partial(body, mesh.shape["row"] // CORES, mesh.shape["col"]),
        mesh=mesh, in_specs=placed, out_specs=P("row", None, "col"), check_vma=False,
    )
```

```python
import functools
import math

import jax
import jax.numpy as jnp
from jax import lax
from jax.experimental import pallas as pl
from jax.experimental.pallas import tpu as pltpu
from jax.sharding import PartitionSpec as P

CORES = 2
CHUNK = 512
SLOTS = 8
LANES = 128
LAG = 3
RING = 2 * LAG + 6
DIRECT = 3
TOP = 32766.0
TINY = 1e-30
LIMIT = 63 * 2**20


def kernel(chips, cols, steps, chunk, sizes, amp, integ, out, raw, gathered, panel, part, peer, stage, inbox,
           scale_out, scale_in, far_stage, far_inbox, far_out, far_in, raw_sem, gather_send, gather_recv, panel_sem, peer_send, peer_recv,
           stage_send, inbox_recv, scale_send, scale_recv, far_send, far_recv, far_scale_send, far_scale_recv):
    row, col = lax.axis_index("row"), lax.axis_index("col")
    z, core = row // CORES, row % CORES
    share, blocks, span = amp.shape
    pairs = share // CORES
    per_block = steps // blocks
    slots, peers, ring = panel.shape[0], peer.shape[0], stage.shape[0]
    relayed = steps - far_stage.shape[0]
    early = min(per_block, slots)
    width = chunk * per_block
    mate = z * CORES + 1 - core
    side = math.isqrt(cols)
    shifts = sorted(((a, b) for a in range(side) for b in range(side) if a or b), key=lambda s: (sum(map(bool, s)), s))

    def partner(shift, sign):
        a, b = (sign * s + side for s in shift)
        return (col // side + a) % side * side + (col % side + b) % side

    def send(src, dst, send_sem, recv_sem, to_row, to_col):
        return pltpu.make_async_remote_copy(
            src_ref=src, dst_ref=dst, send_sem=send_sem, recv_sem=recv_sem,
            device_id={"row": to_row, "col": to_col}, device_id_type=pl.DeviceIdType.MESH)

    def panel_copy(t):
        lanes = pl.ds(pl.multiple_of((t % per_block) * chunk, chunk), chunk)
        slot = t % slots
        return pltpu.make_async_copy(integ.at[t // per_block, :, lanes], panel.at[slot], panel_sem.at[slot])

    raw_copy = pltpu.make_async_copy(amp, raw, raw_sem)

    def gather_copy(h, q, to_col):
        return send(gathered.at[h, q, col], gathered.at[h, q, col], gather_send, gather_recv.at[h, q], row, to_col)

    def peer_copy(t):
        slot = t % peers
        return send(part.at[t, 1 - core], peer.at[slot], peer_send.at[slot], peer_recv.at[slot], mate, col)

    def data_copy(t, way, count, to_row, first):
        slot = t % ring
        return send(stage.at[slot, pl.ds(first, count)], inbox.at[slot, pl.ds(first + 1 - way, count)],
                    stage_send.at[way, slot], inbox_recv.at[way, slot], to_row, col)

    def scale_copy(t, way, to_row):
        slot = t % ring
        return send(scale_out.at[way, slot], scale_in.at[way, slot], scale_send.at[way, slot],
                    scale_recv.at[way, slot], to_row, col)

    def loop(low, high, body):
        lax.fori_loop(low, high, lambda i, c: (body(i), c)[1], 0)

    def when(condition, body, *args):
        @pl.when(condition)
        def _():
            body(*args)

    raw_copy.start()
    for t in range(min(slots, steps)):
        panel_copy(t).start()

    barrier = pltpu.get_barrier_semaphore()

    def greet(to_row, to_col):
        pl.semaphore_signal(barrier, inc=1, device_id={"row": to_row, "col": to_col},
                            device_id_type=pl.DeviceIdType.MESH)

    for shift in shifts:
        greet(row, partner(shift, 1))
    greet(mate, col)
    when(z > 0, greet, row - CORES, col)
    when(z < chips - 1, greet, row + CORES, col)

    def mask(h):
        index = row * span + lax.broadcasted_iota(jnp.int32, (share, span), 1)
        values = jnp.where(index < sizes[h], raw[:, h, :].astype(jnp.float32), 0.0)
        values = values.astype(gathered.dtype)
        for q in range(CORES):
            gathered[h, q, col] = values[q * pairs:(q + 1) * pairs]

    raw_copy.wait()
    mask(0)
    pl.semaphore_wait(barrier, cols + jnp.where(z > 0, 1, 0) + jnp.where(z < chips - 1, 1, 0))

    def scatter(h):
        def one(q):
            for shift in shifts:
                gather_copy(h, q, partner(shift, 1)).start()

        loop(0, CORES, one)

    scatter(0)

    for h in range(1, blocks):
        mask(h)
        scatter(h)

    def collect(h, q):
        others = gathered.at[h, q, pl.ds(0, cols - 1)]
        pltpu.make_async_copy(others, others, gather_recv.at[h, q]).wait()

    def next_panel(t):
        when(t + slots < steps, lambda: panel_copy(t + slots).start())

    def start_peer(t):
        when(t >= peers, lambda: peer_copy(t - peers).wait_send())
        peer_copy(t).start()

    def half(t, q):
        when(t == 0, collect, 0, q)
        when(q == 0, lambda: panel_copy(t).wait())
        left = gathered[0, q].reshape(cols * pairs, span)
        value = jnp.dot(left, panel[t % slots], preferred_element_type=jnp.float32)
        part[t, q] = value.reshape(chips, pairs, chunk)
        when(core != q, start_peer, t)
        when(q == 1, next_panel, t)

    def full(t):
        h = t // per_block
        when(t % per_block == 0, lambda: loop(0, CORES, lambda q: collect(h, q)))
        panel_copy(t).wait()
        left = gathered[h].reshape(CORES * cols * pairs, span)
        value = jnp.dot(left, panel[t % slots], preferred_element_type=jnp.float32)
        part[t] = value.reshape(CORES, chips, pairs, chunk)
        start_peer(t)
        next_panel(t)

    def combine(t):
        peer_copy(t).wait_recv()

        def add(d):
            part[t, core, d] = part[t, core, d] + peer[t % peers, d]

        loop(0, chips, add)

    def fold(value):
        value = jnp.abs(value)
        value = functools.reduce(jnp.maximum, [value[i:i + 8] for i in range(0, pairs, 8)])
        return functools.reduce(jnp.maximum, [value[:, i:i + LANES] for i in range(0, chunk, LANES)])

    def spread(value):
        return jnp.concatenate([value] * (chunk // LANES), axis=1)

    def ahead_of(way):
        return jnp.where(way == 0, chips - 1 - z, z)

    def each_count(count, low, high, body):
        for n in range(low, high):
            when(count == n, body, n)

    def sent_wait(t, way):
        scale_copy(t, way, row).wait_send()
        each_count(ahead_of(way), 1, chips, lambda n: data_copy(t, way, n, row, 0).wait_send())

    def relay(t, way):
        up = way == 0
        has_source = jnp.where(up, z, chips - 1 - z) > 0
        ahead = ahead_of(way)
        to_row = row + CORES - 2 * CORES * way
        first = jnp.where(up, z + 1, 0)
        slot = t % ring

        @pl.when(has_source)
        def _():
            scale_copy(t, way, row).wait_recv()
            each_count(ahead + 1, 1, chips, lambda n: data_copy(t, way, n, row, 0).wait_recv())

        def take(d):
            factor = spread(scale_in[way, slot])
            part[t, core, d] = part[t, core, d] + inbox[slot, d + 1 - way].astype(jnp.int32).astype(jnp.float32) * factor

        when(jnp.logical_and(has_source, ahead > 0), loop, first, first + ahead, take)

        @pl.when(ahead > 0)
        def _():
            when(t >= ring, sent_wait, t - ring, way)
            largest = lax.fori_loop(
                first, first + ahead, lambda d, m: jnp.maximum(m, fold(part[t, core, d])), jnp.full((8, LANES), TINY, jnp.float32))
            largest = jnp.max(largest, axis=0, keepdims=True)
            scale_out[way, slot] = largest * (1.0 / TOP)
            scale_copy(t, way, to_row).start()
            inverse = spread(TOP / largest)

            def put(d):
                stage[slot, d] = jnp.round(part[t, core, d] * inverse).astype(jnp.int32).astype(jnp.int16)

            loop(first, first + ahead, put)
            each_count(ahead, 1, chips, lambda n: data_copy(t, way, n, to_row, first).start())

        when(has_source, take, z)

    def far_copies(t, d):
        slot = t - relayed
        to_row = d * CORES + core
        return (send(far_out.at[slot, d], far_in.at[slot, z], far_scale_send, far_scale_recv.at[slot], to_row, col),
                send(far_stage.at[slot, d], far_inbox.at[slot, z], far_send, far_recv.at[slot], to_row, col))

    def spray(t):
        slot = t - relayed

        def one(j):
            d = jnp.where(2 * z < chips, chips - 1 - j, j)

            @pl.when(d != z)
            def _():
                value = part[t, core, d]
                largest = jnp.max(jnp.maximum(fold(value), TINY), axis=0, keepdims=True)
                far_out[slot, d] = largest * (1.0 / TOP)
                far_stage[slot, d] = jnp.round(value * spread(TOP / largest)).astype(jnp.int32).astype(jnp.int16)
                for copy in far_copies(t, d):
                    copy.start()

        loop(0, chips, one)

    def arrived(t):
        slot = t - relayed
        for box, sem in ((far_in, far_scale_recv), (far_inbox, far_recv)):
            others = box.at[slot, pl.ds(0, chips - 1)]
            pltpu.make_async_copy(others, others, sem.at[slot]).wait()

        def add(source):
            @pl.when(source != z)
            def _():
                value = far_inbox[slot, source].astype(jnp.int32).astype(jnp.float32) * spread(far_in[slot, source])
                part[t, core, z] = part[t, core, z] + value

        loop(0, chips, add)

    def finish(t):
        when(t >= relayed, arrived, t)
        h = t // per_block
        low = (t % per_block) * chunk
        index = col * width + low + lax.broadcasted_iota(jnp.int32, (pairs, chunk), 1)
        out[:, h, pl.ds(pl.multiple_of(low, chunk), chunk)] = jnp.where(index < sizes[h], part[t, core, z], 0.0)

    def at(j, low, high, body):
        ahead = jnp.logical_and(core == 0, j < early)
        t = jnp.where(ahead, j, jnp.where(jnp.logical_and(core == 0, j < 2 * early), -1, j - early))
        when(jnp.logical_and(t >= low, t < high), body, t)

    near = jnp.where(2 * z < chips, 0, 1)
    short = jnp.where(2 * z < chips, z, chips - 1 - z)
    near_lag = 1 + LAG * short
    far_lag = 1 + LAG * (chips - 1 - short)
    end_lag = 1 + LAG * (chips - 1)

    def step(i):
        when(jnp.logical_and(i < 2 * early, i != early), lambda: half(i % early, i // early))
        when(jnp.logical_and(i >= 2 * early, i < steps + early), lambda: full(i - early))
        at(i - 1, 0, steps, combine)
        at(i - 1, relayed, steps, spray)
        at(i - near_lag, 0, relayed, lambda t: relay(t, near))
        at(i - far_lag, 0, relayed, lambda t: relay(t, 1 - near))
        at(i - end_lag, 0, steps, finish)
        when(i == early, lambda: half(0, 1))

    loop(0, steps + early + end_lag, step)

    everything = gathered.at[:, :, pl.ds(0, cols - 1)]
    pltpu.make_async_copy(everything, everything, gather_send).wait()
    loop(max(0, steps - peers), steps, lambda t: peer_copy(t).wait_send())

    def drain(t):
        for way in range(2):
            when(ahead_of(way) > 0, sent_wait, t, way)

    loop(max(0, relayed - ring), relayed, drain)
    for box, sem in ((far_in, far_scale_send), (far_inbox, far_send)):
        others = box.at[:, pl.ds(0, chips - 1)]
        pltpu.make_async_copy(others, others, sem).wait()


def body(chips, cols, amplitudes, integrals, block_sizes):
    share, blocks, span = amplitudes.shape
    width = integrals.shape[2]
    chunk = min(CHUNK, width)
    steps = blocks * (width // chunk)
    total = share * cols
    pairs = total // (chips * CORES)
    assert share == CORES * pairs and chips == cols
    slots = min(SLOTS, steps)
    peers = min(2 * SLOTS, steps)
    ring = min(RING, steps)
    direct = min(DIRECT, steps)
    dma = pltpu.SemaphoreType.DMA
    result = pl.pallas_call(
        functools.partial(kernel, chips, cols, steps, chunk),
        out_shape=jax.ShapeDtypeStruct((pairs, blocks, width), jnp.float32),
        in_specs=[
            pl.BlockSpec(memory_space=pltpu.SMEM),
            pl.BlockSpec(memory_space=pl.ANY),
            pl.BlockSpec(memory_space=pl.ANY),
        ],
        out_specs=pl.BlockSpec(memory_space=pltpu.VMEM),
        scratch_shapes=[
            pltpu.VMEM((share, blocks, span), amplitudes.dtype),
            pltpu.VMEM((blocks, CORES, cols, pairs, span), amplitudes.dtype),
            pltpu.VMEM((slots, span, chunk), integrals.dtype),
            pltpu.VMEM((steps, CORES, chips, pairs, chunk), jnp.float32),
            pltpu.VMEM((peers, chips, pairs, chunk), jnp.float32),
            pltpu.VMEM((ring, chips, pairs, chunk), jnp.int16),
            pltpu.VMEM((ring, chips + 1, pairs, chunk), jnp.int16),
            pltpu.VMEM((2, ring, 1, LANES), jnp.float32),
            pltpu.VMEM((2, ring, 1, LANES), jnp.float32),
            pltpu.VMEM((direct, chips, pairs, chunk), jnp.int16),
            pltpu.VMEM((direct, chips, pairs, chunk), jnp.int16),
            pltpu.VMEM((direct, chips, 1, LANES), jnp.float32),
            pltpu.VMEM((direct, chips, 1, LANES), jnp.float32),
            dma,
            dma,
            dma((blocks, CORES)),
            dma((slots,)),
            dma((peers,)),
            dma((peers,)),
            dma((2, ring)),
            dma((2, ring)),
            dma((2, ring)),
            dma((2, ring)),
            dma,
            dma((direct,)),
            dma,
            dma((direct,)),
        ],
        compiler_params=pltpu.CompilerParams(
            collective_id=0, has_side_effects=True, vmem_limit_bytes=LIMIT
        ),
        name="ladder",
    )(block_sizes, amplitudes, integrals)
    return result


def solution(mesh):
    placed = (P("col", None, "row"), P(None, "row", "col"), P())
    return jax.shard_map(
        functools.partial(body, mesh.shape["row"] // CORES, mesh.shape["col"]),
        mesh=mesh, in_specs=placed, out_specs=P("row", None, "col"), check_vma=False,
    )
```
